32 devices in a mesh: lon: 8 (over z, x), lat: 4 (over y, core).
Axes of the slice: x: 2, y: 2, z: 4, core: 2. Of those that a mesh axis runs over, the one named last changes fastest.
Arguments:
- efield_north: float32 [128, 3072], P('lat', 'lon'), may hold values from -13 to 14
- efield_east: float32 [128, 3072], P('lat', 'lon'), may hold values from -13 to 14
- efield_up: float32 [128, 3072], P('lat', 'lon'), may hold values from -13 to 14
- hfield_north: float32 [128, 3072], P('lat', 'lon'), may hold values from -13 to 14
- hfield_east: float32 [128, 3072], P('lat', 'lon'), may hold values from -13 to 14
- hfield_up: float32 [128, 3072], P('lat', 'lon'), may hold values from -13 to 14
- sigma_profile: float32 [24], replicated, may hold values from 0.001 to 30
- flash_lat: int32 [64], replicated, may hold values from 0 to 126
- flash_lon: int32 [64], replicated, may hold values from 0 to 127
- flash_step: int32 [64], replicated, may hold values from 0 to 8
- flash_amp: float32 [64], replicated, may hold values from 20 to 60
Outputs:
- electric_north: float32 [128, 3072], P('lat', 'lon')
- electric_east: float32 [128, 3072], P('lat', 'lon')
- electric_up: float32 [128, 3072], P('lat', 'lon')
- magnetic_north: float32 [128, 3072], P('lat', 'lon')
- magnetic_east: float32 [128, 3072], P('lat', 'lon')
- magnetic_up: float32 [128, 3072], P('lat', 'lon')
- zonal_means: float32 [9, 2, 128, 24], P(None, None, 'lat')
The draws below stay inside these ranges and needn't reach their ends.
All inputs are finite; a program needn't handle non-finite values.
Results may differ from the reference program's by a relative error of at most 0.0003.
Values sent between devices are 32-bit elements; how exact they have to be, the bound alone decides.
A program may use at most 64 MiB of HBM per device.

```python
import math
import jax
import jax.numpy as jnp
from jax import lax

ALT = 24
CHANNEL = 3
STEPS = 9
FLASHES = 64
NLON = 128
NLAT = 128


def field_draw(key, salt_value):
    inner_key = jax.random.fold_in(key, salt_value)
    rough_key, scale_key = jax.random.split(inner_key)
    field_shape = (NLAT, NLON, ALT)
    spread = jnp.exp(jax.random.uniform(scale_key, field_shape, jnp.float32, math.log(0.3), math.log(3.0)))
    lon_place = (jnp.arange(NLON, dtype=jnp.float32) / NLON)[None, :, None]
    rough_part = jax.random.truncated_normal(rough_key, -4.0, 4.0, field_shape, jnp.float32)
    background = 0.5 + lon_place
    return (rough_part * spread + background).reshape(NLAT, NLON * ALT)


def draw_efield_north(key, part):
    return field_draw(key, 11)


def draw_efield_east(key, part):
    return field_draw(key, 12)


def draw_efield_up(key, part):
    return field_draw(key, 13)


def draw_hfield_north(key, part):
    return field_draw(key, 21)


def draw_hfield_east(key, part):
    return field_draw(key, 22)


def draw_hfield_up(key, part):
    return field_draw(key, 23)


def with_ends(entries, own_key, smallest, largest):
    spot = [jax.random.randint(jax.random.fold_in(own_key, axis), (), 0, length) for axis, length in enumerate(entries.shape)]
    main_axis = entries.shape.index(max(entries.shape))
    beside = spot[:main_axis] + [(spot[main_axis] + 1) % entries.shape[main_axis]] + spot[main_axis + 1:]
    return entries.at[tuple(spot)].set(smallest).at[tuple(beside)].set(largest)


def setup_inputs(seed: int = 0) -> dict:
    keys = jax.random.split(jax.random.key(seed), 12)
    return {
        "efield_north": draw_efield_north(jax.random.fold_in(keys[11], 71), 0),
        "efield_east": draw_efield_east(jax.random.fold_in(keys[11], 71), 0),
        "efield_up": draw_efield_up(jax.random.fold_in(keys[11], 71), 0),
        "hfield_north": draw_hfield_north(jax.random.fold_in(keys[11], 71), 0),
        "hfield_east": draw_hfield_east(jax.random.fold_in(keys[11], 71), 0),
        "hfield_up": draw_hfield_up(jax.random.fold_in(keys[11], 71), 0),
        "sigma_profile": jnp.clip(jnp.exp(jax.random.uniform(keys[6], (ALT,), jnp.float32, math.log(0.001), math.log(30.0))), 0.001, 30.0),
        "flash_lat": with_ends(jax.random.randint(keys[7], (FLASHES,), 0, NLAT - 1), jax.random.fold_in(keys[7], 1), 0, (NLAT - 1) - 1).astype(jnp.int32),
        "flash_lon": with_ends(jax.random.randint(keys[8], (FLASHES,), 0, NLON), jax.random.fold_in(keys[8], 1), 0, NLON - 1).astype(jnp.int32),
        "flash_step": with_ends(jax.random.randint(keys[9], (FLASHES,), 0, STEPS), jax.random.fold_in(keys[9], 1), 0, STEPS - 1).astype(jnp.int32),
        "flash_amp": jnp.clip(jax.random.uniform(keys[10], (FLASHES,), jnp.float32, 20.0, 60.0), 20.0, 60.0),
    }


RADIUS_CELLS = 1529.0
COURANT = 0.9

def time_step(lat_count, lon_count):
    lon_angle = 2.0 * math.pi / lon_count
    lat_angle = math.pi / lat_count
    narrowest = RADIUS_CELLS * lon_angle * math.sin(lat_angle)
    lat_length = RADIUS_CELLS * lat_angle
    return COURANT / math.sqrt(1.0 / narrowest ** 2 + 1.0 / lat_length ** 2 + 1.0)

def grid_terms(row_index, lat_count, lon_count):
    lon_angle = 2.0 * math.pi / lon_count
    lat_angle = math.pi / lat_count
    row_place = row_index.astype(jnp.float32)
    centre = -0.5 * math.pi + (row_place + 0.5) * lat_angle
    north_edge = centre + 0.5 * lat_angle
    south_edge = centre - 0.5 * lat_angle
    next_centre = centre + lat_angle
    at_pole = row_index == lat_count - 1
    at_south = row_index == 0
    scale_lon = RADIUS_CELLS * lon_angle
    band_area = 2.0 * RADIUS_CELLS * scale_lon * math.sin(0.5 * lat_angle)
    span_centre = scale_lon * jnp.cos(centre)
    span_next = scale_lon * jnp.cos(next_centre)
    span_edge = jnp.where(at_pole, 0.0, scale_lon * jnp.cos(north_edge))
    span_south = jnp.where(at_south, 0.0, scale_lon * jnp.cos(south_edge))
    area_centre = band_area * jnp.cos(centre)
    area_edge = jnp.where(at_pole, 1.0, band_area * jnp.cos(north_edge))
    safe_edge = jnp.where(at_pole, 1.0, span_edge)
    keeper = jnp.where(at_pole, 0.0, 1.0)
    return (span_centre, span_next, span_edge, span_south, area_centre, area_edge, safe_edge, keeper)

def level_above(values):
    return jnp.concatenate([values[1:], jnp.zeros_like(values[:1])], axis=0)

def level_below(values):
    return jnp.concatenate([jnp.zeros_like(values[:1]), values[:-1]], axis=0)

def from_south(values):
    return jnp.concatenate([jnp.zeros_like(values[:, :1]), values[:, :-1]], axis=1)

def from_north(values):
    return jnp.concatenate([values[:, 1:], jnp.zeros_like(values[:, :1])], axis=1)

def reference(efield_north, efield_east, efield_up, hfield_north, hfield_east, hfield_up, sigma_profile, flash_lat, flash_lon, flash_step, flash_amp):
    lat_count = efield_north.shape[0]
    lon_count = efield_north.shape[1] // ALT

    def to_cube(flat_field):
        return flat_field.reshape(lat_count, lon_count, ALT).transpose(2, 0, 1)

    def to_flat(cube_field):
        return cube_field.transpose(1, 2, 0).reshape(lat_count, lon_count * ALT)
    time_delta = time_step(lat_count, lon_count)
    lat_length = RADIUS_CELLS * math.pi / lat_count
    row_index = jnp.arange(lat_count, dtype=jnp.int32)
    metric_terms = [metric_term[None, :, None] for metric_term in grid_terms(row_index, lat_count, lon_count)]
    span_centre, span_next, span_edge, span_south, area_centre, area_edge, safe_edge, keeper = metric_terms
    half_loss = 0.5 * time_delta * sigma_profile
    decay_factor = ((1.0 - half_loss) / (1.0 + half_loss))[:, None, None]
    drive_factor = (time_delta / (1.0 + half_loss))[:, None, None]
    channel = (jnp.arange(ALT) < CHANNEL).astype(jnp.float32)[:, None, None]
    south_row = (row_index == 0)[None, :, None]
    north_row = (row_index == lat_count - 1)[None, :, None]
    e_north = to_cube(efield_north)
    e_east = keeper * to_cube(efield_east)
    e_up = keeper * to_cube(efield_up)
    h_north = keeper * to_cube(hfield_north)
    h_east = to_cube(hfield_east)
    h_up = to_cube(hfield_up)
    history = []
    for step_index in range(STEPS):
        mean_east = lax.optimization_barrier(jnp.mean(e_east, axis=2))
        mean_up = lax.optimization_barrier(jnp.mean(h_up, axis=2))
        history.append(jnp.stack([mean_east, mean_up]))
        north_next = jnp.roll(e_north, -1, axis=2)
        up_next = jnp.roll(e_up, -1, axis=2)
        circulation = span_south * from_south(e_east) - span_edge * e_east + lat_length * (north_next - e_north)
        up_new = h_up - time_delta * circulation / area_centre
        south_cap = mean_up[:, 0] + time_delta * span_edge[0, 0, 0] * mean_east[:, 0] / area_centre[0, 0, 0]
        north_cap = mean_up[:, -1] - time_delta * span_edge[0, -2, 0] * mean_east[:, -2] / area_centre[0, -1, 0]
        up_new = jnp.where(south_row, south_cap[:, None, None], up_new)
        up_new = jnp.where(north_row, north_cap[:, None, None], up_new)
        north_new = keeper * (h_north - time_delta * ((e_up - up_next) / safe_edge + level_above(e_east) - e_east))
        east_new = h_east - time_delta * ((e_up - from_south(e_up)) / lat_length - (level_above(e_north) - e_north))
        h_up, h_north, h_east = (up_new, north_new, east_new)
        e_north_new = decay_factor * e_north + drive_factor * (h_east - level_below(h_east) - (h_up - jnp.roll(h_up, 1, axis=2)) / span_centre)
        e_east_new = keeper * (decay_factor * e_east + drive_factor * ((from_north(h_up) - h_up) / lat_length - (h_north - level_below(h_north))))
        loop_flux = span_centre * h_east - span_next * from_north(h_east) + lat_length * (h_north - jnp.roll(h_north, 1, axis=2))
        strike = (flash_step == step_index).astype(jnp.float32) * flash_amp
        source = jnp.zeros((lat_count, lon_count), jnp.float32).at[flash_lat, flash_lon].add(strike)
        e_up_new = keeper * (decay_factor * e_up + drive_factor * loop_flux / area_edge) + drive_factor * channel * source[None]
        e_north, e_east, e_up = (e_north_new, e_east_new, e_up_new)
    zonal_out = jnp.stack(history).transpose(0, 1, 3, 2)
    return (to_flat(e_north), to_flat(e_east), to_flat(e_up), to_flat(h_north), to_flat(h_east), to_flat(h_up), zonal_out)
```

```python
import functools
import math

import jax
import jax.numpy as jnp
import numpy as np
from jax import lax
from jax.experimental import pallas as pl
from jax.experimental.pallas import tpu as pltpu
from jax.sharding import PartitionSpec as P

CHANNEL = 3
STEPS = 9
RADIUS_CELLS = 1529.0
COURANT = 0.9

HALO_ROWS = 8
HALO_LANES = 128
PAD = 8
FIRST = 5
MESH = pl.DeviceIdType.MESH
DIRECTIONS = [(a, b) for a in (-1, 0, 1) for b in (-1, 0, 1) if (a, b) != (0, 0)]
EN, EE, EU, HN, HE, HR = range(6)
(C_AS, C_BE, C_CN, C_DU, C_DT, C_GC, C_IC, C_JN, C_KL, C_LY) = range(10)
C_KEEP = 10


def time_step(lat_count, lon_count):
    lon_angle = 2.0 * math.pi / lon_count
    lat_angle = math.pi / lat_count
    narrowest = RADIUS_CELLS * lon_angle * math.sin(lat_angle)
    lat_length = RADIUS_CELLS * lat_angle
    return COURANT / math.sqrt(1.0 / narrowest**2 + 1.0 / lat_length**2 + 1.0)


def row_table(lat_count, lon_count):
    f = np.float32
    lon_angle = 2.0 * math.pi / lon_count
    lat_angle = math.pi / lat_count
    dt = time_step(lat_count, lon_count)
    ly = RADIUS_CELLS * math.pi / lat_count
    row = np.arange(lat_count)
    centre = f(-0.5 * math.pi) + (row.astype(f) + f(0.5)) * f(lat_angle)
    north = centre + f(0.5 * lat_angle)
    south = centre - f(0.5 * lat_angle)
    following = centre + f(lat_angle)
    pole = row == lat_count - 1
    scale = RADIUS_CELLS * lon_angle
    band = 2.0 * RADIUS_CELLS * scale * math.sin(0.5 * lat_angle)
    lc = f(scale) * np.cos(centre)
    ln = f(scale) * np.cos(following)
    le = np.where(pole, f(0), f(scale) * np.cos(north))
    ls = np.where(row == 0, f(0), f(scale) * np.cos(south))
    ls[-1] = le[-2]
    ac = f(band) * np.cos(centre)
    ae = np.where(pole, f(1), f(band) * np.cos(north))
    se = np.where(pole, f(1), le)
    keep = np.where(pole, f(0), f(1))
    table = np.zeros((lat_count + 2 * HALO_ROWS, 128), f)
    inner = table[HALO_ROWS:-HALO_ROWS]
    inner[:, C_AS] = dt * ls / ac
    inner[:, C_BE] = dt * le / ac
    inner[:, C_CN] = dt * ly / ac
    inner[:, C_DU] = keep * dt / se
    inner[:, C_DT] = keep * dt
    inner[:, C_GC] = 1.0 / lc
    inner[:, C_IC] = keep * lc / ae
    inner[:, C_JN] = keep * ln / ae
    inner[:, C_KL] = keep * ly / ae
    inner[:, C_LY] = keep / ly
    inner[:, C_KEEP] = keep
    return table


def turn(x, by):
    return pltpu.roll(x, by % x.shape[1], 1)


def div24(x):
    return lax.shift_right_logical(x * 2731, 16)


def kernel(
    dims,
    en, ee, eu, hn, he, hr, sigma, f_lat, f_lon, f_step, f_amp, table,
    o_en, o_ee, o_eu, o_hn, o_he, o_hr, o_zon,
    ext_a, ext_b, coef, lanes, src, small, sums_out, sums_in, zon_cap, zon_out, strip,
    send_a, recv_a, send_b, recv_b, send_s, recv_s, send_z, recv_z,
):
    n_lat, n_lon, layers, dt, ly = dims
    rows, width = en.shape
    wide = width + 2 * HALO_LANES
    tall = rows + 2 * HALO_ROWS
    groups = tall // 8
    vregs = wide // 128
    lat, lon = lax.axis_index("lat"), lax.axis_index("lon")
    own_r = pl.ds(PAD + HALO_ROWS, rows)
    own_c = pl.ds(HALO_LANES, width)

    def at(a, b):
        row = jnp.clip(lat + a, 0, n_lat - 1) if a else lat
        return {"lat": row, "lon": lax.rem(lon + b + n_lon, n_lon)}

    def there(a):
        return lat + a >= 0 if a < 0 else lat + a < n_lat

    def guarded(a, fn):
        if a == 0:
            fn()
        else:
            pl.when(there(a))(fn)

    barrier = pltpu.get_barrier_semaphore()

    def greet(a, b):
        pl.semaphore_signal(barrier, inc=1, device_id=at(a, b), device_id_type=MESH)

    for k in range(1, n_lon):
        greet(0, k)
    for a in (-1, 1):
        def both(a=a):
            for b in (-1, 0, 1):
                greet(a, b)
        pl.when(there(a))(both)

    keep = table[pl.ds(lat * rows + HALO_ROWS, rows), C_KEEP:C_KEEP + 1]
    keep = jnp.broadcast_to(keep, (rows, width))
    start = [en[...], keep * ee[...], keep * eu[...], keep * hn[...], he[...], hr[...]]
    low = PAD + HALO_ROWS
    for ext in (ext_a, ext_b):
        edge = jnp.zeros((6, 8, wide), jnp.float32)
        ext[:, 0:PAD, :] = edge
        ext[:, low + rows + 8:, :] = edge
        for a, first_row in ((-1, PAD), (1, low + rows)):
            def clear(ext=ext, first_row=first_row):
                ext[:, first_row:first_row + 8, :] = jnp.zeros((6, 8, wide), jnp.float32)
            pl.when(jnp.logical_not(there(a)))(clear)
    for f in range(6):
        ext_a[f, own_r, own_c] = start[f]

    def fold(x):
        for by in (width // 2, width // 4, width // 8, width // 16):
            x = x + turn(x, by)
        return x[:, :128] * (1.0 / (n_lon * (width // layers)))

    lane = lax.broadcasted_iota(jnp.int32, (rows, 128), 1)
    sums_out[...] = jnp.where(
        lane < layers,
        fold(start[EE]),
        jnp.where(lane < 2 * layers, fold(start[HN]), fold(start[HR])),
    )

    greeted = (n_lon - 1) + 3 * (lat > 0).astype(jnp.int32) + 3 * (lat < n_lat - 1).astype(jnp.int32)
    pl.semaphore_wait(barrier, greeted)

    def strip_copy(src_ref, dst_ref, sends, recvs, i):
        a, b = DIRECTIONS[i]
        def part(first, size, halo, d, side):
            if d == 0:
                return pl.ds(first, size)
            if side == 0:
                return pl.ds(first + size - halo, halo) if d > 0 else pl.ds(first, halo)
            return pl.ds(first - halo, halo) if d > 0 else pl.ds(first + size, halo)
        def cut(side):
            return (
                slice(None),
                part(PAD + HALO_ROWS, rows, HALO_ROWS, a, side),
                part(HALO_LANES, width, HALO_LANES, b, side),
            )
        return pltpu.make_async_remote_copy(
            src_ref=src_ref.at[cut(0)],
            dst_ref=dst_ref.at[cut(1)],
            send_sem=sends.at[i],
            recv_sem=recvs.at[i],
            device_id=at(a, b),
            device_id_type=MESH,
        )

    def start_all(*args):
        for i, (a, b) in enumerate(DIRECTIONS):
            guarded(a, lambda i=i: strip_copy(*args, i).start())

    def wait_sends(*args):
        for i, (a, b) in enumerate(DIRECTIONS):
            guarded(a, lambda i=i: strip_copy(*args, i).wait_send())

    def wait_recvs(*args):
        for i, (a, b) in enumerate(DIRECTIONS):
            guarded(-a, lambda i=i: strip_copy(*args, i).wait_recv())

    first = (ext_a, ext_a, send_a, recv_a)
    second = (ext_a, ext_b, send_b, recv_b)

    def sum_copy(k):
        return pltpu.make_async_remote_copy(
            src_ref=sums_out,
            dst_ref=sums_in.at[k],
            send_sem=send_s.at[k],
            recv_sem=recv_s.at[k],
            device_id=at(0, k),
            device_id_type=MESH,
        )

    start_all(*first)
    for k in range(1, n_lon):
        sum_copy(k).start()

    rows_tab = table[pl.ds(lat * rows, tall), :]
    for c in range(10):
        coef[c] = jnp.broadcast_to(rows_tab[:, c:c + 1], (tall, 128))
    small[...] = jnp.zeros((8, 128), jnp.float32)
    small[0:1, 0:layers] = sigma[...]
    one = jnp.broadcast_to(small[0:1, :], (8, 128))
    pair = one + turn(one, 24)
    sig = pair + turn(pair, 48) + turn(one, 96)
    half = 0.5 * dt * sig
    dec = (1.0 - half) / (1.0 + half)
    drv = dt / (1.0 + half)
    lane8 = lax.broadcasted_iota(jnp.int32, (8, 128), 1)

    def spread(x):
        out = []
        for v in range(vregs):
            off = (8 * v - 8) % 24
            out.append(jnp.where(lane8 < 96, turn(x, -off), turn(x, 24 - off)))
        return jnp.concatenate(out, axis=1)

    at_lane = lax.broadcasted_iota(jnp.int32, (8, wide), 1) + 16
    layer = at_lane - 24 * div24(at_lane)
    lanes[0] = spread(dec)
    lanes[1] = spread(drv)
    lanes[2] = jnp.where(layer < CHANNEL, lanes[1], 0.0)
    lanes[3] = jnp.where(layer == layers - 1, 0.0, 1.0)
    lanes[4] = jnp.where(layer == 0, 0.0, 1.0)

    strokes = f_lat.shape[1]
    place = lax.broadcasted_iota(jnp.int32, (wide, strokes), 0) + 16
    cell = div24(place) - 6 + lon * (width // layers)
    total_lon = n_lon * (width // layers)
    cell = jnp.where(cell < 0, cell + total_lon, cell)
    cell = jnp.where(cell >= total_lon, cell - total_lon, cell)
    cells = (cell == f_lon[...]).astype(jnp.float32).astype(jnp.bfloat16)
    row_no = lax.broadcasted_iota(jnp.int32, (tall, strokes), 0) + (lat * rows - HALO_ROWS)
    in_row = jnp.where(row_no == f_lat[...], jnp.broadcast_to(f_amp[...], (tall, strokes)), 0.0)
    def sources(s, carry):
        amps = jnp.where(f_step[...] == s, in_row, 0.0)
        total = None
        for _ in range(3):
            part = amps.astype(jnp.bfloat16)
            amps = amps - part.astype(jnp.float32)
            term = lax.dot_general(
                part, cells, (((1,), (1,)), ((), ())), preferred_element_type=jnp.float32
            )
            total = term if total is None else total + term
        src[pl.ds(pl.multiple_of(s * tall, 8), tall), :] = total
        return carry
    lax.fori_loop(0, STEPS, sources, 0)

    for k in range(1, n_lon):
        sum_copy(k).wait()
    mean = sums_out[...]
    for k in range(1, n_lon):
        mean = mean + sums_in[k]
    strip[own_r, :] = mean
    strip[0:low, :] = jnp.zeros((low, 128), jnp.float32)

    def zone_copy(a):
        i = 0 if a < 0 else 1
        return pltpu.make_async_remote_copy(
            src_ref=strip.at[pl.ds(low, 8) if a < 0 else pl.ds(low + rows - 8, 8), :],
            dst_ref=sums_in.at[0, pl.ds(8, 8) if a < 0 else pl.ds(0, 8), :],
            send_sem=send_z.at[i],
            recv_sem=recv_z.at[i],
            device_id=at(a, 0),
            device_id_type=MESH,
        )

    for a in (-1, 1):
        guarded(a, lambda a=a: zone_copy(a).start())

    def unpack(x):
        out = []
        lane_no = lax.broadcasted_iota(jnp.int32, x.shape, 1)
        for f in range(3):
            y = jnp.where(lane_no < layers, turn(x, -layers * f), 0.0)
            p = y + turn(y, 24)
            out.append(p + turn(p, 48) + turn(y, 96))
        return out

    zero_low = jnp.zeros((3, low, 128), jnp.float32)
    zon_cap[:, 0:low, :] = zero_low
    zon_cap[:, low + rows:, :] = zero_low
    zon_out[:, 0:low, :] = zero_low
    zon_out[:, low + rows:, :] = zero_low
    for f, z in enumerate(unpack(mean)):
        zon_cap[f, own_r, :] = z
        zon_out[f, own_r, :] = z

    z_dec, z_drv, z_top, z_bot = [lanes.at[i, :, 128:256] for i in (0, 1, 3, 4)]

    def zonal_step(zon, span):
        for g in span:
            lo, r = PAD + 8 * g, 8 * g
            east = zon[0, lo:lo + 8, :]
            zon[2, lo:lo + 8, :] = (
                zon[2, lo:lo + 8, :]
                - coef[C_AS, r:r + 8] * zon[0, lo - 1:lo + 7, :]
                + coef[C_BE, r:r + 8] * east
            )
            zon[1, lo:lo + 8, :] = zon[1, lo:lo + 8, :] - coef[C_DT, r:r + 8] * (
                z_top[...] * turn(east, -1) - east
            )
        for g in span:
            lo, r = PAD + 8 * g, 8 * g
            up, north = zon[2, lo:lo + 8, :], zon[1, lo:lo + 8, :]
            zon[0, lo:lo + 8, :] = z_dec[...] * zon[0, lo:lo + 8, :] + z_drv[...] * (
                coef[C_LY, r:r + 8] * (zon[2, lo + 1:lo + 9, :] - up)
                - (north - z_bot[...] * turn(north, 1))
            )

    def rowc(c, g):
        return jnp.concatenate([coef[c, 8 * g:8 * g + 8]] * vregs, axis=1)

    def step(ext, s):
        zonal_step(zon_cap, range(1, groups - 1))
        for g in range(groups):
            lo = PAD + 8 * g
            here = slice(lo, lo + 8)
            south = slice(lo - 1, lo + 7)
            top = lanes[3]
            e_n, e_e, e_u = ext[EN, here], ext[EE, here], ext[EU, here]
            up = (
                ext[HR, here]
                - rowc(C_AS, g) * ext[EE, south]
                + rowc(C_BE, g) * e_e
                - rowc(C_CN, g) * (turn(e_n, -layers) - e_n)
            )
            if g in (1, groups - 2):
                row = lax.broadcasted_iota(jnp.int32, (8, wide), 0) + (lat * rows - HALO_ROWS + 8 * g)
                pole = 0 if g == 1 else n_lat * rows - 1
                up = jnp.where(row == pole, spread(zon_cap[2, here]), up)
            ext[HR, here] = up
            ext[HN, here] = (
                ext[HN, here]
                - rowc(C_DU, g) * (e_u - turn(e_u, -layers))
                - rowc(C_DT, g) * (top * turn(e_e, -1) - e_e)
            )
            ext[HE, here] = (
                ext[HE, here]
                - (dt / ly) * (e_u - ext[EU, south])
                + dt * (top * turn(e_n, -1) - e_n)
            )
        for g in range(groups):
            lo = PAD + 8 * g
            here = slice(lo, lo + 8)
            north = slice(lo + 1, lo + 9)
            decay, drive, channel, bot = lanes[0], lanes[1], lanes[2], lanes[4]
            h_n, h_e, h_r = ext[HN, here], ext[HE, here], ext[HR, here]
            ext[EN, here] = decay * ext[EN, here] + drive * (
                h_e - bot * turn(h_e, 1) - rowc(C_GC, g) * (h_r - turn(h_r, layers))
            )
            ext[EE, here] = decay * ext[EE, here] + drive * (
                rowc(C_LY, g) * (ext[HR, north] - h_r) - (h_n - bot * turn(h_n, 1))
            )
            ext[EU, here] = (
                decay * ext[EU, here]
                + drive
                * (
                    rowc(C_IC, g) * h_e
                    - rowc(C_JN, g) * ext[HE, north]
                    + rowc(C_KL, g) * (h_n - turn(h_n, layers))
                )
                + channel * src[pl.ds(pl.multiple_of(s * tall + 8 * g, 8), 8), :]
            )

    def steps(ext, begin, end):
        def one_step(s, carry):
            step(ext, s)
            return carry
        lax.fori_loop(begin, end, one_step, 0)

    wait_recvs(*first)
    wait_sends(*first)
    steps(ext_a, 0, FIRST)
    start_all(*second)
    ext_b[:, own_r, own_c] = ext_a[:, own_r, own_c]

    for a in (-1, 1):
        def take(a=a):
            zone_copy(a).wait_recv()
            side = unpack(sums_in[0, 0:8, :] if a > 0 else sums_in[0, 8:16, :])
            for f in range(3):
                if a > 0:
                    zon_out[f, PAD:low, :] = side[f]
                else:
                    zon_out[f, low + rows:low + rows + 8, :] = side[f]
        guarded(-a, take)
        guarded(a, lambda a=a: zone_copy(a).wait_send())

    def record(s, carry):
        o_zon[s, 0] = zon_out[0, own_r, 0:layers]
        o_zon[s, 1] = zon_out[2, own_r, 0:layers]
        zonal_step(zon_out, range(groups))
        return carry
    lax.fori_loop(0, STEPS, record, 0)

    wait_recvs(*second)
    steps(ext_b, FIRST, STEPS)
    for f, out in ((EN, o_en), (EE, o_ee), (EU, o_eu), (HN, o_hn), (HE, o_he), (HR, o_hr)):
        out[...] = ext_b[f, own_r, own_c]
    wait_sends(*second)


def body(
    efield_north,
    efield_east,
    efield_up,
    hfield_north,
    hfield_east,
    hfield_up,
    sigma_profile,
    flash_lat,
    flash_lon,
    flash_step,
    flash_amp,
):
    rows, width = efield_north.shape
    layers = sigma_profile.shape[0]
    n_lat, n_lon = lax.axis_size("lat"), lax.axis_size("lon")
    lat_count, lon_count = rows * n_lat, (width // layers) * n_lon
    dims = (
        n_lat,
        n_lon,
        layers,
        time_step(lat_count, lon_count),
        RADIUS_CELLS * math.pi / lat_count,
    )
    wide, tall = width + 2 * HALO_LANES, rows + 2 * HALO_ROWS
    f32 = jnp.float32
    vmem = pl.BlockSpec(memory_space=pltpu.VMEM)
    field = jax.ShapeDtypeStruct((rows, width), f32)
    dma = pltpu.SemaphoreType.DMA
    return pl.pallas_call(
        functools.partial(kernel, dims),
        out_shape=[field] * 6 + [jax.ShapeDtypeStruct((STEPS, 2, rows, layers), f32)],
        in_specs=[vmem] * 12,
        out_specs=[vmem] * 7,
        scratch_shapes=[
            pltpu.VMEM((6, tall + 2 * PAD, wide), f32),
            pltpu.VMEM((6, tall + 2 * PAD, wide), f32),
            pltpu.VMEM((10, tall, 128), f32),
            pltpu.VMEM((5, 8, wide), f32),
            pltpu.VMEM((STEPS * tall, wide), f32),
            pltpu.VMEM((8, 128), f32),
            pltpu.VMEM((rows, 128), f32),
            pltpu.VMEM((n_lon, rows, 128), f32),
            pltpu.VMEM((3, tall + 2 * PAD, 128), f32),
            pltpu.VMEM((3, tall + 2 * PAD, 128), f32),
            pltpu.VMEM((tall + 2 * PAD, 128), f32),
            dma((8,)), dma((8,)), dma((8,)), dma((8,)),
            dma((n_lon,)), dma((n_lon,)), dma((2,)), dma((2,)),
        ],
        compiler_params=pltpu.CompilerParams(
            collective_id=0, has_side_effects=True, vmem_limit_bytes=32 * 1024 * 1024
        ),
    )(
        efield_north,
        efield_east,
        efield_up,
        hfield_north,
        hfield_east,
        hfield_up,
        sigma_profile[None, :],
        flash_lat[None, :],
        flash_lon[None, :],
        flash_step[None, :],
        flash_amp[None, :],
        jnp.asarray(row_table(lat_count, lon_count)),
    )


def solution(mesh):
    fields = P("lat", "lon")
    return jax.shard_map(
        body,
        mesh=mesh,
        in_specs=(fields,) * 6 + (P(),) * 5,
        out_specs=(fields,) * 6 + (P(None, None, "lat", None),),
        check_vma=False,
    )
```

```python
import functools
import math

import jax
import jax.numpy as jnp
import numpy as np
from jax import lax
from jax.experimental import pallas as pl
from jax.experimental.pallas import tpu as pltpu
from jax.sharding import PartitionSpec as P

CHANNEL = 3
STEPS = 9
RADIUS_CELLS = 1529.0
COURANT = 0.9
VMEM_GRANT = 63 * 1024 * 1024

HALO_ROWS = 8
HALO_LANES = 128
PAD = 8
FIRST = 5
MESH = pl.DeviceIdType.MESH
DIRECTIONS = [(a, b) for a in (-1, 0, 1) for b in (-1, 0, 1) if (a, b) != (0, 0)]
EN, EE, EU, HN, HE, HR = range(6)
(C_AS, C_BE, C_CN, C_DU, C_DT, C_GC, C_IC, C_JN, C_KL, C_LY) = range(10)
C_KEEP = 10


def time_step(lat_count, lon_count):
    lon_angle = 2.0 * math.pi / lon_count
    lat_angle = math.pi / lat_count
    narrowest = RADIUS_CELLS * lon_angle * math.sin(lat_angle)
    lat_length = RADIUS_CELLS * lat_angle
    return COURANT / math.sqrt(1.0 / narrowest**2 + 1.0 / lat_length**2 + 1.0)


def row_table(lat_count, lon_count):
    f = np.float32
    lon_angle = 2.0 * math.pi / lon_count
    lat_angle = math.pi / lat_count
    dt = time_step(lat_count, lon_count)
    ly = RADIUS_CELLS * math.pi / lat_count
    row = np.arange(lat_count)
    centre = f(-0.5 * math.pi) + (row.astype(f) + f(0.5)) * f(lat_angle)
    north = centre + f(0.5 * lat_angle)
    south = centre - f(0.5 * lat_angle)
    following = centre + f(lat_angle)
    pole = row == lat_count - 1
    scale = RADIUS_CELLS * lon_angle
    band = 2.0 * RADIUS_CELLS * scale * math.sin(0.5 * lat_angle)
    lc = f(scale) * np.cos(centre)
    ln = f(scale) * np.cos(following)
    le = np.where(pole, f(0), f(scale) * np.cos(north))
    ls = np.where(row == 0, f(0), f(scale) * np.cos(south))
    ls[-1] = le[-2]
    ac = f(band) * np.cos(centre)
    ae = np.where(pole, f(1), f(band) * np.cos(north))
    se = np.where(pole, f(1), le)
    keep = np.where(pole, f(0), f(1))
    table = np.zeros((lat_count + 2 * HALO_ROWS, 128), f)
    inner = table[HALO_ROWS:-HALO_ROWS]
    inner[:, C_AS] = dt * ls / ac
    inner[:, C_BE] = dt * le / ac
    inner[:, C_CN] = dt * ly / ac
    inner[:, C_DU] = keep * dt / se
    inner[:, C_DT] = keep * dt
    inner[:, C_GC] = 1.0 / lc
    inner[:, C_IC] = keep * lc / ae
    inner[:, C_JN] = keep * ln / ae
    inner[:, C_KL] = keep * ly / ae
    inner[:, C_LY] = keep / ly
    inner[:, C_KEEP] = keep
    return table


def turn(x, by):
    return pltpu.roll(x, by % x.shape[1], 1)


def div24(x):
    return lax.shift_right_logical(x * 2731, 16)


def kernel(
    dims,
    en, ee, eu, hn, he, hr, h_sigma, h_lat, h_lon, h_step, h_amp, h_table,
    o_en, o_ee, o_eu, o_hn, o_he, o_hr, o_zon,
    ext_a, ext_b, coef, lanes, src, small, sums_out, sums_in, zon_cap, zon_out, strip,
    sigma, f_lat, f_lon, f_step, f_amp, table,
    load, send_a, recv_a, send_b, recv_b, send_s, recv_s, send_z, recv_z,
):
    n_lat, n_lon, layers, dt, ly = dims
    rows, width = en.shape
    strokes = h_lat.shape[1]
    wide = width + 2 * HALO_LANES
    tall = rows + 2 * HALO_ROWS
    groups = tall // 8
    vregs = wide // 128
    lat, lon = lax.axis_index("lat"), lax.axis_index("lon")
    own_r = pl.ds(PAD + HALO_ROWS, rows)
    own_c = pl.ds(HALO_LANES, width)

    def at(a, b):
        row = jnp.clip(lat + a, 0, n_lat - 1) if a else lat
        return {"lat": row, "lon": lax.rem(lon + b + n_lon, n_lon)}

    def there(a):
        return lat + a >= 0 if a < 0 else lat + a < n_lat

    def guarded(a, fn):
        if a == 0:
            fn()
        else:
            pl.when(there(a))(fn)

    loads = [
        pltpu.make_async_copy(x, ext_a.at[f, own_r, own_c], load.at[f])
        for f, x in enumerate((en, ee, eu, hn, he, hr))
    ]
    here_rows = h_table.at[pl.ds(pl.multiple_of(lat * rows, 8), tall), :]
    pairs = (
        (here_rows, table), (h_sigma, sigma), (h_lat, f_lat), (h_lon, f_lon),
        (h_step, f_step), (h_amp, f_amp),
    )
    loads += [pltpu.make_async_copy(x, y, load.at[6 + i]) for i, (x, y) in enumerate(pairs)]
    for copy in loads:
        copy.start()

    barrier = pltpu.get_barrier_semaphore()

    def greet(a, b):
        pl.semaphore_signal(barrier, inc=1, device_id=at(a, b), device_id_type=MESH)

    for k in range(1, n_lon):
        greet(0, k)
    for a in (-1, 1):
        def both(a=a):
            for b in (-1, 0, 1):
                greet(a, b)
        pl.when(there(a))(both)

    low = PAD + HALO_ROWS
    for ext in (ext_a, ext_b):
        edge = jnp.zeros((6, 8, wide), jnp.float32)
        ext[:, 0:PAD, :] = edge
        ext[:, low + rows + 8:, :] = edge
        for a, first_row in ((-1, PAD), (1, low + rows)):
            def clear(ext=ext, first_row=first_row):
                ext[:, first_row:first_row + 8, :] = jnp.zeros((6, 8, wide), jnp.float32)
            pl.when(jnp.logical_not(there(a)))(clear)
    for copy in loads:
        copy.wait()
    last = pl.ds(low + rows - 8, 8)
    keep = jnp.broadcast_to(table[HALO_ROWS + rows - 8:HALO_ROWS + rows, C_KEEP:C_KEEP + 1], (8, width))
    for f in (EE, EU, HN):
        ext_a[f, last, own_c] = keep * ext_a[f, last, own_c]

    def fold(x):
        for by in (width // 2, width // 4, width // 8, width // 16):
            x = x + turn(x, by)
        return x[:, :128] * (1.0 / (n_lon * (width // layers)))

    lane = lax.broadcasted_iota(jnp.int32, (rows, 128), 1)
    sums_out[...] = jnp.where(
        lane < layers,
        fold(ext_a[EE, own_r, own_c]),
        jnp.where(lane < 2 * layers, fold(ext_a[HN, own_r, own_c]), fold(ext_a[HR, own_r, own_c])),
    )

    greeted = (n_lon - 1) + 3 * (lat > 0).astype(jnp.int32) + 3 * (lat < n_lat - 1).astype(jnp.int32)
    pl.semaphore_wait(barrier, greeted)

    def strip_copy(src_ref, dst_ref, sends, recvs, i):
        a, b = DIRECTIONS[i]
        def part(first, size, halo, d, side):
            if d == 0:
                return pl.ds(first, size)
            if side == 0:
                return pl.ds(first + size - halo, halo) if d > 0 else pl.ds(first, halo)
            return pl.ds(first - halo, halo) if d > 0 else pl.ds(first + size, halo)
        def cut(side):
            return (
                slice(None),
                part(PAD + HALO_ROWS, rows, HALO_ROWS, a, side),
                part(HALO_LANES, width, HALO_LANES, b, side),
            )
        return pltpu.make_async_remote_copy(
            src_ref=src_ref.at[cut(0)],
            dst_ref=dst_ref.at[cut(1)],
            send_sem=sends.at[i],
            recv_sem=recvs.at[i],
            device_id=at(a, b),
            device_id_type=MESH,
        )

    def start_all(*args):
        for i, (a, b) in enumerate(DIRECTIONS):
            guarded(a, lambda i=i: strip_copy(*args, i).start())

    def wait_sends(*args):
        for i, (a, b) in enumerate(DIRECTIONS):
            guarded(a, lambda i=i: strip_copy(*args, i).wait_send())

    def wait_recvs(*args):
        for i, (a, b) in enumerate(DIRECTIONS):
            guarded(-a, lambda i=i: strip_copy(*args, i).wait_recv())

    first = (ext_a, ext_a, send_a, recv_a)
    second = (ext_a, ext_b, send_b, recv_b)

    def sum_copy(k):
        return pltpu.make_async_remote_copy(
            src_ref=sums_out,
            dst_ref=sums_in.at[k],
            send_sem=send_s.at[k],
            recv_sem=recv_s.at[k],
            device_id=at(0, k),
            device_id_type=MESH,
        )

    start_all(*first)
    for k in range(1, n_lon):
        sum_copy(k).start()

    rows_tab = table[...]
    for c in range(10):
        coef[c] = jnp.broadcast_to(rows_tab[:, c:c + 1], (tall, 128))
    small[...] = jnp.zeros((8, 128), jnp.float32)
    small[0:1, 0:layers] = sigma[...]
    one = jnp.broadcast_to(small[0:1, :], (8, 128))
    pair = one + turn(one, 24)
    sig = pair + turn(pair, 48) + turn(one, 96)
    half = 0.5 * dt * sig
    dec = (1.0 - half) / (1.0 + half)
    drv = dt / (1.0 + half)
    lane8 = lax.broadcasted_iota(jnp.int32, (8, 128), 1)

    def spread(x):
        out = []
        for v in range(vregs):
            off = (8 * v - 8) % 24
            out.append(jnp.where(lane8 < 96, turn(x, -off), turn(x, 24 - off)))
        return jnp.concatenate(out, axis=1)

    at_lane = lax.broadcasted_iota(jnp.int32, (8, wide), 1) + 16
    layer = at_lane - 24 * div24(at_lane)
    lanes[0] = spread(dec)
    lanes[1] = spread(drv)
    lanes[2] = jnp.where(layer < CHANNEL, lanes[1], 0.0)
    lanes[3] = jnp.where(layer == layers - 1, 0.0, 1.0)
    lanes[4] = jnp.where(layer == 0, 0.0, 1.0)

    place = lax.broadcasted_iota(jnp.int32, (wide, strokes), 0) + 16
    cell = div24(place) - 6 + lon * (width // layers)
    total_lon = n_lon * (width // layers)
    cell = jnp.where(cell < 0, cell + total_lon, cell)
    cell = jnp.where(cell >= total_lon, cell - total_lon, cell)
    cells = (cell == f_lon[...]).astype(jnp.float32).astype(jnp.bfloat16)
    row_no = lax.broadcasted_iota(jnp.int32, (tall, strokes), 0) + (lat * rows - HALO_ROWS)
    in_row = jnp.where(row_no == f_lat[...], jnp.broadcast_to(f_amp[...], (tall, strokes)), 0.0)
    def sources(s, carry):
        amps = jnp.where(f_step[...] == s, in_row, 0.0)
        total = None
        for _ in range(3):
            part = amps.astype(jnp.bfloat16)
            amps = amps - part.astype(jnp.float32)
            term = lax.dot_general(
                part, cells, (((1,), (1,)), ((), ())), preferred_element_type=jnp.float32
            )
            total = term if total is None else total + term
        src[pl.ds(pl.multiple_of(s * tall, 8), tall), :] = total
        return carry
    lax.fori_loop(0, STEPS, sources, 0)

    for k in range(1, n_lon):
        sum_copy(k).wait()
    mean = sums_out[...]
    for k in range(1, n_lon):
        mean = mean + sums_in[k]
    strip[own_r, :] = mean
    strip[0:low, :] = jnp.zeros((low, 128), jnp.float32)

    def zone_copy(a):
        i = 0 if a < 0 else 1
        return pltpu.make_async_remote_copy(
            src_ref=strip.at[pl.ds(low, 8) if a < 0 else pl.ds(low + rows - 8, 8), :],
            dst_ref=sums_in.at[0, pl.ds(8, 8) if a < 0 else pl.ds(0, 8), :],
            send_sem=send_z.at[i],
            recv_sem=recv_z.at[i],
            device_id=at(a, 0),
            device_id_type=MESH,
        )

    for a in (-1, 1):
        guarded(a, lambda a=a: zone_copy(a).start())

    def unpack(x):
        out = []
        lane_no = lax.broadcasted_iota(jnp.int32, x.shape, 1)
        for f in range(3):
            y = jnp.where(lane_no < layers, turn(x, -layers * f), 0.0)
            p = y + turn(y, 24)
            out.append(p + turn(p, 48) + turn(y, 96))
        return out

    zero_low = jnp.zeros((3, low, 128), jnp.float32)
    zon_cap[:, 0:low, :] = zero_low
    zon_cap[:, low + rows:, :] = zero_low
    zon_out[:, 0:low, :] = zero_low
    zon_out[:, low + rows:, :] = zero_low
    for f, z in enumerate(unpack(mean)):
        zon_cap[f, own_r, :] = z
        zon_out[f, own_r, :] = z

    z_dec, z_drv, z_top, z_bot = [lanes.at[i, :, 128:256] for i in (0, 1, 3, 4)]

    def zonal_step(zon, span):
        for g in span:
            lo, r = PAD + 8 * g, 8 * g
            east = zon[0, lo:lo + 8, :]
            zon[2, lo:lo + 8, :] = (
                zon[2, lo:lo + 8, :]
                - coef[C_AS, r:r + 8] * zon[0, lo - 1:lo + 7, :]
                + coef[C_BE, r:r + 8] * east
            )
            zon[1, lo:lo + 8, :] = zon[1, lo:lo + 8, :] - coef[C_DT, r:r + 8] * (
                z_top[...] * turn(east, -1) - east
            )
        for g in span:
            lo, r = PAD + 8 * g, 8 * g
            up, north = zon[2, lo:lo + 8, :], zon[1, lo:lo + 8, :]
            zon[0, lo:lo + 8, :] = z_dec[...] * zon[0, lo:lo + 8, :] + z_drv[...] * (
                coef[C_LY, r:r + 8] * (zon[2, lo + 1:lo + 9, :] - up)
                - (north - z_bot[...] * turn(north, 1))
            )

    def rowc(c, g):
        return jnp.concatenate([coef[c, 8 * g:8 * g + 8]] * vregs, axis=1)

    def step(ext, s):
        zonal_step(zon_cap, range(1, groups - 1))
        for g in range(groups):
            lo = PAD + 8 * g
            here = slice(lo, lo + 8)
            south = slice(lo - 1, lo + 7)
            top = lanes[3]
            e_n, e_e, e_u = ext[EN, here], ext[EE, here], ext[EU, here]
            up = (
                ext[HR, here]
                - rowc(C_AS, g) * ext[EE, south]
                + rowc(C_BE, g) * e_e
                - rowc(C_CN, g) * (turn(e_n, -layers) - e_n)
            )
            if g in (1, groups - 2):
                row = lax.broadcasted_iota(jnp.int32, (8, wide), 0) + (lat * rows - HALO_ROWS + 8 * g)
                pole = 0 if g == 1 else n_lat * rows - 1
                up = jnp.where(row == pole, spread(zon_cap[2, here]), up)
            ext[HR, here] = up
            ext[HN, here] = (
                ext[HN, here]
                - rowc(C_DU, g) * (e_u - turn(e_u, -layers))
                - rowc(C_DT, g) * (top * turn(e_e, -1) - e_e)
            )
            ext[HE, here] = (
                ext[HE, here]
                - (dt / ly) * (e_u - ext[EU, south])
                + dt * (top * turn(e_n, -1) - e_n)
            )
        for g in range(groups):
            lo = PAD + 8 * g
            here = slice(lo, lo + 8)
            north = slice(lo + 1, lo + 9)
            decay, drive, channel, bot = lanes[0], lanes[1], lanes[2], lanes[4]
            h_n, h_e, h_r = ext[HN, here], ext[HE, here], ext[HR, here]
            ext[EN, here] = decay * ext[EN, here] + drive * (
                h_e - bot * turn(h_e, 1) - rowc(C_GC, g) * (h_r - turn(h_r, layers))
            )
            ext[EE, here] = decay * ext[EE, here] + drive * (
                rowc(C_LY, g) * (ext[HR, north] - h_r) - (h_n - bot * turn(h_n, 1))
            )
            ext[EU, here] = (
                decay * ext[EU, here]
                + drive
                * (
                    rowc(C_IC, g) * h_e
                    - rowc(C_JN, g) * ext[HE, north]
                    + rowc(C_KL, g) * (h_n - turn(h_n, layers))
                )
                + channel * src[pl.ds(pl.multiple_of(s * tall + 8 * g, 8), 8), :]
            )

    def steps(ext, begin, end):
        def one_step(s, carry):
            step(ext, s)
            return carry
        lax.fori_loop(begin, end, one_step, 0)

    wait_recvs(*first)
    wait_sends(*first)
    steps(ext_a, 0, FIRST)
    start_all(*second)
    ext_b[:, own_r, own_c] = ext_a[:, own_r, own_c]

    for a in (-1, 1):
        def take(a=a):
            zone_copy(a).wait_recv()
            side = unpack(sums_in[0, 0:8, :] if a > 0 else sums_in[0, 8:16, :])
            for f in range(3):
                if a > 0:
                    zon_out[f, PAD:low, :] = side[f]
                else:
                    zon_out[f, low + rows:low + rows + 8, :] = side[f]
        guarded(-a, take)
        guarded(a, lambda a=a: zone_copy(a).wait_send())

    def record(s, carry):
        both = jnp.where(lane < layers, zon_out[0, own_r, :], turn(zon_out[2, own_r, :], layers))
        both = jnp.transpose(both)
        o_zon[s, 0] = both[0:layers]
        o_zon[s, 1] = both[layers:2 * layers]
        zonal_step(zon_out, range(groups))
        return carry
    lax.fori_loop(0, STEPS, record, 0)

    wait_recvs(*second)
    steps(ext_b, FIRST, STEPS)
    for f, out in ((EN, o_en), (EE, o_ee), (EU, o_eu), (HN, o_hn), (HE, o_he), (HR, o_hr)):
        out[...] = ext_b[f, own_r, own_c]
    wait_sends(*second)


def hand_over(*refs):
    count = len(refs) // 2
    sems = refs[-1]
    copies = [
        pltpu.make_async_copy(refs[i], refs[count + i], sems.at[i]) for i in range(count)
    ]
    for copy in copies:
        copy.start()
    for copy in copies:
        copy.wait()


def body(
    efield_north,
    efield_east,
    efield_up,
    hfield_north,
    hfield_east,
    hfield_up,
    sigma_profile,
    flash_lat,
    flash_lon,
    flash_step,
    flash_amp,
):
    rows, width = efield_north.shape
    layers = sigma_profile.shape[0]
    n_lat, n_lon = lax.axis_size("lat"), lax.axis_size("lon")
    lat_count, lon_count = rows * n_lat, (width // layers) * n_lon
    dims = (
        n_lat,
        n_lon,
        layers,
        time_step(lat_count, lon_count),
        RADIUS_CELLS * math.pi / lat_count,
    )
    wide, tall = width + 2 * HALO_LANES, rows + 2 * HALO_ROWS
    f32 = jnp.float32
    vmem = pl.BlockSpec(memory_space=pltpu.VMEM)
    field = jax.ShapeDtypeStruct((rows, width), f32)
    dma = pltpu.SemaphoreType.DMA
    hbm = pl.BlockSpec(memory_space=pltpu.HBM)
    strokes = flash_lat.shape[0]
    outs = [field] * 6 + [jax.ShapeDtypeStruct((STEPS, 2, layers, rows), f32)]
    results = pl.pallas_call(
        functools.partial(kernel, dims),
        out_shape=outs,
        in_specs=[hbm] * 12,
        out_specs=[vmem] * 7,
        scratch_shapes=[
            pltpu.VMEM((6, tall + 2 * PAD, wide), f32),
            pltpu.VMEM((6, tall + 2 * PAD, wide), f32),
            pltpu.VMEM((10, tall, 128), f32),
            pltpu.VMEM((5, 8, wide), f32),
            pltpu.VMEM((STEPS * tall, wide), f32),
            pltpu.VMEM((8, 128), f32),
            pltpu.VMEM((rows, 128), f32),
            pltpu.VMEM((n_lon, rows, 128), f32),
            pltpu.VMEM((3, tall + 2 * PAD, 128), f32),
            pltpu.VMEM((3, tall + 2 * PAD, 128), f32),
            pltpu.VMEM((tall + 2 * PAD, 128), f32),
            pltpu.VMEM((1, layers), f32),
            pltpu.VMEM((1, strokes), jnp.int32),
            pltpu.VMEM((1, strokes), jnp.int32),
            pltpu.VMEM((1, strokes), jnp.int32),
            pltpu.VMEM((1, strokes), f32),
            pltpu.VMEM((tall, 128), f32),
            dma((12,)),
            dma((8,)), dma((8,)), dma((8,)), dma((8,)),
            dma((n_lon,)), dma((n_lon,)), dma((2,)), dma((2,)),
        ],
        compiler_params=pltpu.CompilerParams(
            collective_id=0, has_side_effects=True, vmem_limit_bytes=VMEM_GRANT
        ),
    )(
        efield_north,
        efield_east,
        efield_up,
        hfield_north,
        hfield_east,
        hfield_up,
        sigma_profile[None, :],
        flash_lat[None, :],
        flash_lon[None, :],
        flash_step[None, :],
        flash_amp[None, :],
        jnp.asarray(row_table(lat_count, lon_count)),
    )
    results = pl.pallas_call(
        hand_over,
        out_shape=outs,
        in_specs=[hbm] * 7,
        out_specs=[hbm] * 7,
        scratch_shapes=[dma((7,))],
        compiler_params=pltpu.CompilerParams(vmem_limit_bytes=VMEM_GRANT),
    )(*results)
    return (*results[:6], jnp.transpose(results[6], (0, 1, 3, 2)))


def solution(mesh):
    fields = P("lat", "lon")
    return jax.shard_map(
        body,
        mesh=mesh,
        in_specs=(fields,) * 6 + (P(),) * 5,
        out_specs=(fields,) * 6 + (P(None, None, "lat", None),),
        check_vma=False,
    )
```

```python
import functools
import math

import jax
import jax.numpy as jnp
import numpy as np
from jax import lax
from jax.experimental import pallas as pl
from jax.experimental.pallas import tpu as pltpu
from jax.sharding import PartitionSpec as P

CHANNEL = 3
STEPS = 9
RADIUS_CELLS = 1529.0
COURANT = 0.9
VMEM_GRANT = 63 * 1024 * 1024

HALO_ROWS = 8
HALO_LANES = 128
PAD = 8
FIRST = 5
MESH = pl.DeviceIdType.MESH
DIRECTIONS = [(a, b) for a in (-1, 0, 1) for b in (-1, 0, 1) if (a, b) != (0, 0)]
EN, EE, EU, HN, HE, HR = range(6)
(C_AS, C_BE, C_CN, C_DU, C_DT, C_GC, C_IC, C_JN, C_KL, C_LY) = range(10)
C_KEEP = 10


def time_step(lat_count, lon_count):
    lon_angle = 2.0 * math.pi / lon_count
    lat_angle = math.pi / lat_count
    narrowest = RADIUS_CELLS * lon_angle * math.sin(lat_angle)
    lat_length = RADIUS_CELLS * lat_angle
    return COURANT / math.sqrt(1.0 / narrowest**2 + 1.0 / lat_length**2 + 1.0)


def row_table(lat_count, lon_count):
    f = np.float32
    lon_angle = 2.0 * math.pi / lon_count
    lat_angle = math.pi / lat_count
    dt = time_step(lat_count, lon_count)
    ly = RADIUS_CELLS * math.pi / lat_count
    row = np.arange(lat_count)
    centre = f(-0.5 * math.pi) + (row.astype(f) + f(0.5)) * f(lat_angle)
    north = centre + f(0.5 * lat_angle)
    south = centre - f(0.5 * lat_angle)
    following = centre + f(lat_angle)
    pole = row == lat_count - 1
    scale = RADIUS_CELLS * lon_angle
    band = 2.0 * RADIUS_CELLS * scale * math.sin(0.5 * lat_angle)
    lc = f(scale) * np.cos(centre)
    ln = f(scale) * np.cos(following)
    le = np.where(pole, f(0), f(scale) * np.cos(north))
    ls = np.where(row == 0, f(0), f(scale) * np.cos(south))
    ls[-1] = le[-2]
    ac = f(band) * np.cos(centre)
    ae = np.where(pole, f(1), f(band) * np.cos(north))
    se = np.where(pole, f(1), le)
    keep = np.where(pole, f(0), f(1))
    table = np.zeros((lat_count + 2 * HALO_ROWS, 128), f)
    inner = table[HALO_ROWS:-HALO_ROWS]
    inner[:, C_AS] = dt * ls / ac
    inner[:, C_BE] = dt * le / ac
    inner[:, C_CN] = dt * ly / ac
    inner[:, C_DU] = keep * dt / se
    inner[:, C_DT] = keep * dt
    inner[:, C_GC] = 1.0 / lc
    inner[:, C_IC] = keep * lc / ae
    inner[:, C_JN] = keep * ln / ae
    inner[:, C_KL] = keep * ly / ae
    inner[:, C_LY] = keep / ly
    inner[:, C_KEEP] = keep
    return table


def turn(x, by):
    return pltpu.roll(x, by % x.shape[1], 1)


def div24(x):
    return lax.shift_right_logical(x * 2731, 16)


def kernel(
    dims,
    en, ee, eu, hn, he, hr, h_sigma, h_lat, h_lon, h_step, h_amp, h_table,
    o_en, o_ee, o_eu, o_hn, o_he, o_hr, o_zon,
    ext_a, ext_b, coef, lanes, src, small, sums_out, sums_in, zon_cap, zon_out, strip,
    sigma, f_lat, f_lon, f_step, f_amp, table,
    load, send_a, recv_a, send_b, recv_b, send_s, recv_s, send_z, recv_z,
):
    n_lat, n_lon, layers, dt, ly = dims
    rows, width = en.shape
    strokes = h_lat.shape[1]
    wide = width + 2 * HALO_LANES
    tall = rows + 2 * HALO_ROWS
    groups = tall // 8
    vregs = wide // 128
    lat, lon = lax.axis_index("lat"), lax.axis_index("lon")
    own_r = pl.ds(PAD + HALO_ROWS, rows)
    own_c = pl.ds(HALO_LANES, width)

    def at(a, b):
        row = jnp.clip(lat + a, 0, n_lat - 1) if a else lat
        return {"lat": row, "lon": lax.rem(lon + b + n_lon, n_lon)}

    def there(a):
        return lat + a >= 0 if a < 0 else lat + a < n_lat

    def guarded(a, fn):
        if a == 0:
            fn()
        else:
            pl.when(there(a))(fn)

    loads = [
        pltpu.make_async_copy(x, ext_a.at[f, own_r, own_c], load.at[f])
        for f, x in enumerate((en, ee, eu, hn, he, hr))
    ]
    here_rows = h_table.at[pl.ds(pl.multiple_of(lat * rows, 8), tall), :]
    pairs = (
        (here_rows, table), (h_sigma, sigma), (h_lat, f_lat), (h_lon, f_lon),
        (h_step, f_step), (h_amp, f_amp),
    )
    loads += [pltpu.make_async_copy(x, y, load.at[6 + i]) for i, (x, y) in enumerate(pairs)]
    for copy in loads:
        copy.start()

    barrier = pltpu.get_barrier_semaphore()

    def greet(a, b):
        pl.semaphore_signal(barrier, inc=1, device_id=at(a, b), device_id_type=MESH)

    for k in range(1, n_lon):
        greet(0, k)
    for a in (-1, 1):
        def both(a=a):
            for b in (-1, 0, 1):
                greet(a, b)
        pl.when(there(a))(both)

    low = PAD + HALO_ROWS
    for ext in (ext_a, ext_b):
        edge = jnp.zeros((6, 8, wide), jnp.float32)
        ext[:, 0:PAD, :] = edge
        ext[:, low + rows + 8:, :] = edge
        for a, first_row in ((-1, PAD), (1, low + rows)):
            def clear(ext=ext, first_row=first_row):
                ext[:, first_row:first_row + 8, :] = jnp.zeros((6, 8, wide), jnp.float32)
            pl.when(jnp.logical_not(there(a)))(clear)
    for copy in loads:
        copy.wait()
    last = pl.ds(low + rows - 8, 8)
    keep = jnp.broadcast_to(table[HALO_ROWS + rows - 8:HALO_ROWS + rows, C_KEEP:C_KEEP + 1], (8, width))
    for f in (EE, EU, HN):
        ext_a[f, last, own_c] = keep * ext_a[f, last, own_c]

    def fold(x):
        for by in (width // 2, width // 4, width // 8, width // 16):
            x = x + turn(x, by)
        return x[:, :128] * (1.0 / (n_lon * (width // layers)))

    lane = lax.broadcasted_iota(jnp.int32, (rows, 128), 1)
    sums_out[...] = jnp.where(
        lane < layers,
        fold(ext_a[EE, own_r, own_c]),
        jnp.where(lane < 2 * layers, fold(ext_a[HN, own_r, own_c]), fold(ext_a[HR, own_r, own_c])),
    )

    greeted = (n_lon - 1) + 3 * (lat > 0).astype(jnp.int32) + 3 * (lat < n_lat - 1).astype(jnp.int32)
    pl.semaphore_wait(barrier, greeted)

    def strip_copy(src_ref, dst_ref, sends, recvs, i):
        a, b = DIRECTIONS[i]
        def part(first, size, halo, d, side):
            if d == 0:
                return pl.ds(first, size)
            if side == 0:
                return pl.ds(first + size - halo, halo) if d > 0 else pl.ds(first, halo)
            return pl.ds(first - halo, halo) if d > 0 else pl.ds(first + size, halo)
        def cut(side):
            return (
                slice(None),
                part(PAD + HALO_ROWS, rows, FIRST, a, side),
                part(HALO_LANES, width, HALO_LANES, b, side),
            )
        return pltpu.make_async_remote_copy(
            src_ref=src_ref.at[cut(0)],
            dst_ref=dst_ref.at[cut(1)],
            send_sem=sends.at[i],
            recv_sem=recvs.at[i],
            device_id=at(a, b),
            device_id_type=MESH,
        )

    def start_all(*args):
        for i, (a, b) in enumerate(DIRECTIONS):
            guarded(a, lambda i=i: strip_copy(*args, i).start())

    def wait_sends(*args):
        for i, (a, b) in enumerate(DIRECTIONS):
            guarded(a, lambda i=i: strip_copy(*args, i).wait_send())

    def wait_recvs(*args):
        for i, (a, b) in enumerate(DIRECTIONS):
            guarded(-a, lambda i=i: strip_copy(*args, i).wait_recv())

    first = (ext_a, ext_a, send_a, recv_a)
    second = (ext_a, ext_b, send_b, recv_b)

    def sum_copy(k):
        return pltpu.make_async_remote_copy(
            src_ref=sums_out,
            dst_ref=sums_in.at[k],
            send_sem=send_s.at[k],
            recv_sem=recv_s.at[k],
            device_id=at(0, k),
            device_id_type=MESH,
        )

    for k in range(1, n_lon):
        sum_copy(k).start()
    start_all(*first)

    rows_tab = table[...]
    for c in range(10):
        coef[c] = jnp.broadcast_to(rows_tab[:, c:c + 1], (tall, 128))
    small[...] = jnp.zeros((8, 128), jnp.float32)
    small[0:1, 0:layers] = sigma[...]
    one = jnp.broadcast_to(small[0:1, :], (8, 128))
    pair = one + turn(one, 24)
    sig = pair + turn(pair, 48) + turn(one, 96)
    half = 0.5 * dt * sig
    dec = (1.0 - half) / (1.0 + half)
    drv = dt / (1.0 + half)
    lane8 = lax.broadcasted_iota(jnp.int32, (8, 128), 1)

    def spread(x):
        out = []
        for v in range(vregs):
            off = (8 * v - 8) % 24
            out.append(jnp.where(lane8 < 96, turn(x, -off), turn(x, 24 - off)))
        return jnp.concatenate(out, axis=1)

    at_lane = lax.broadcasted_iota(jnp.int32, (8, wide), 1) + 16
    layer = at_lane - 24 * div24(at_lane)
    lanes[0] = spread(dec)
    lanes[1] = spread(drv)
    lanes[2] = jnp.where(layer < CHANNEL, lanes[1], 0.0)
    lanes[3] = jnp.where(layer == layers - 1, 0.0, 1.0)
    lanes[4] = jnp.where(layer == 0, 0.0, 1.0)

    place = lax.broadcasted_iota(jnp.int32, (wide, strokes), 0) + 16
    cell = div24(place) - 6 + lon * (width // layers)
    total_lon = n_lon * (width // layers)
    cell = jnp.where(cell < 0, cell + total_lon, cell)
    cell = jnp.where(cell >= total_lon, cell - total_lon, cell)
    cells = (cell == f_lon[...]).astype(jnp.float32).astype(jnp.bfloat16)
    row_no = lax.broadcasted_iota(jnp.int32, (tall, strokes), 0) + (lat * rows - HALO_ROWS)
    in_row = jnp.where(row_no == f_lat[...], jnp.broadcast_to(f_amp[...], (tall, strokes)), 0.0)
    def sources(s, carry):
        amps = jnp.where(f_step[...] == s, in_row, 0.0)
        total = None
        for _ in range(3):
            part = amps.astype(jnp.bfloat16)
            amps = amps - part.astype(jnp.float32)
            term = lax.dot_general(
                part, cells, (((1,), (1,)), ((), ())), preferred_element_type=jnp.float32
            )
            total = term if total is None else total + term
        src[pl.ds(pl.multiple_of(s * tall, 8), tall), :] = total
        return carry
    lax.fori_loop(0, STEPS, sources, 0)

    for k in range(1, n_lon):
        sum_copy(k).wait()
    mean = sums_out[...]
    for k in range(1, n_lon):
        mean = mean + sums_in[k]
    strip[own_r, :] = mean
    strip[0:low, :] = jnp.zeros((low, 128), jnp.float32)

    def zone_copy(a):
        i = 0 if a < 0 else 1
        return pltpu.make_async_remote_copy(
            src_ref=strip.at[pl.ds(low, 8) if a < 0 else pl.ds(low + rows - 8, 8), :],
            dst_ref=sums_in.at[0, pl.ds(8, 8) if a < 0 else pl.ds(0, 8), :],
            send_sem=send_z.at[i],
            recv_sem=recv_z.at[i],
            device_id=at(a, 0),
            device_id_type=MESH,
        )

    for a in (-1, 1):
        guarded(a, lambda a=a: zone_copy(a).start())

    def unpack(x):
        out = []
        lane_no = lax.broadcasted_iota(jnp.int32, x.shape, 1)
        for f in range(3):
            y = jnp.where(lane_no < layers, turn(x, -layers * f), 0.0)
            p = y + turn(y, 24)
            out.append(p + turn(p, 48) + turn(y, 96))
        return out

    zero_low = jnp.zeros((3, low, 128), jnp.float32)
    zon_cap[:, 0:low, :] = zero_low
    zon_cap[:, low + rows:, :] = zero_low
    zon_out[:, 0:low, :] = zero_low
    zon_out[:, low + rows:, :] = zero_low
    for f, z in enumerate(unpack(mean)):
        zon_cap[f, own_r, :] = z
        zon_out[f, own_r, :] = z

    z_dec, z_drv, z_top, z_bot = [lanes.at[i, :, 128:256] for i in (0, 1, 3, 4)]

    def zonal_step(zon, span):
        for g in span:
            lo, r = PAD + 8 * g, 8 * g
            east = zon[0, lo:lo + 8, :]
            zon[2, lo:lo + 8, :] = (
                zon[2, lo:lo + 8, :]
                - coef[C_AS, r:r + 8] * zon[0, lo - 1:lo + 7, :]
                + coef[C_BE, r:r + 8] * east
            )
            zon[1, lo:lo + 8, :] = zon[1, lo:lo + 8, :] - coef[C_DT, r:r + 8] * (
                z_top[...] * turn(east, -1) - east
            )
        for g in span:
            lo, r = PAD + 8 * g, 8 * g
            up, north = zon[2, lo:lo + 8, :], zon[1, lo:lo + 8, :]
            zon[0, lo:lo + 8, :] = z_dec[...] * zon[0, lo:lo + 8, :] + z_drv[...] * (
                coef[C_LY, r:r + 8] * (zon[2, lo + 1:lo + 9, :] - up)
                - (north - z_bot[...] * turn(north, 1))
            )

    def rowc(c, g):
        return jnp.concatenate([coef[c, 8 * g:8 * g + 8]] * vregs, axis=1)

    def step(ext, s):
        zonal_step(zon_cap, range(1, groups - 1))
        for g in range(groups):
            lo = PAD + 8 * g
            here = slice(lo, lo + 8)
            south = slice(lo - 1, lo + 7)
            top = lanes[3]
            e_n, e_e, e_u = ext[EN, here], ext[EE, here], ext[EU, here]
            up = (
                ext[HR, here]
                - rowc(C_AS, g) * ext[EE, south]
                + rowc(C_BE, g) * e_e
                - rowc(C_CN, g) * (turn(e_n, -layers) - e_n)
            )
            if g in (1, groups - 2):
                row = lax.broadcasted_iota(jnp.int32, (8, wide), 0) + (lat * rows - HALO_ROWS + 8 * g)
                pole = 0 if g == 1 else n_lat * rows - 1
                up = jnp.where(row == pole, spread(zon_cap[2, here]), up)
            ext[HR, here] = up
            ext[HN, here] = (
                ext[HN, here]
                - rowc(C_DU, g) * (e_u - turn(e_u, -layers))
                - rowc(C_DT, g) * (top * turn(e_e, -1) - e_e)
            )
            ext[HE, here] = (
                ext[HE, here]
                - (dt / ly) * (e_u - ext[EU, south])
                + dt * (top * turn(e_n, -1) - e_n)
            )
        for g in range(groups):
            lo = PAD + 8 * g
            here = slice(lo, lo + 8)
            north = slice(lo + 1, lo + 9)
            decay, drive, channel, bot = lanes[0], lanes[1], lanes[2], lanes[4]
            h_n, h_e, h_r = ext[HN, here], ext[HE, here], ext[HR, here]
            ext[EN, here] = decay * ext[EN, here] + drive * (
                h_e - bot * turn(h_e, 1) - rowc(C_GC, g) * (h_r - turn(h_r, layers))
            )
            ext[EE, here] = decay * ext[EE, here] + drive * (
                rowc(C_LY, g) * (ext[HR, north] - h_r) - (h_n - bot * turn(h_n, 1))
            )
            ext[EU, here] = (
                decay * ext[EU, here]
                + drive
                * (
                    rowc(C_IC, g) * h_e
                    - rowc(C_JN, g) * ext[HE, north]
                    + rowc(C_KL, g) * (h_n - turn(h_n, layers))
                )
                + channel * src[pl.ds(pl.multiple_of(s * tall + 8 * g, 8), 8), :]
            )

    def steps(ext, begin, end):
        def one_step(s, carry):
            step(ext, s)
            return carry
        lax.fori_loop(begin, end, one_step, 0)

    wait_recvs(*first)
    wait_sends(*first)
    steps(ext_a, 0, FIRST)
    start_all(*second)
    ext_b[:, own_r, own_c] = ext_a[:, own_r, own_c]

    for a in (-1, 1):
        def take(a=a):
            zone_copy(a).wait_recv()
            side = unpack(sums_in[0, 0:8, :] if a > 0 else sums_in[0, 8:16, :])
            for f in range(3):
                if a > 0:
                    zon_out[f, PAD:low, :] = side[f]
                else:
                    zon_out[f, low + rows:low + rows + 8, :] = side[f]
        guarded(-a, take)
        guarded(a, lambda a=a: zone_copy(a).wait_send())

    def record(s, carry):
        both = jnp.where(lane < layers, zon_out[0, own_r, :], turn(zon_out[2, own_r, :], layers))
        both = jnp.transpose(both)
        o_zon[s, 0] = both[0:layers]
        o_zon[s, 1] = both[layers:2 * layers]
        zonal_step(zon_out, range(groups))
        return carry
    lax.fori_loop(0, STEPS, record, 0)

    wait_recvs(*second)
    steps(ext_b, FIRST, STEPS)
    for f, out in ((EN, o_en), (EE, o_ee), (EU, o_eu), (HN, o_hn), (HE, o_he), (HR, o_hr)):
        out[...] = ext_b[f, own_r, own_c]
    wait_sends(*second)


def hand_over(*refs):
    count = len(refs) // 3
    sources, results, held, sems = refs[:count], refs[count:2 * count], refs[2 * count:-1], refs[-1]
    ins = [pltpu.make_async_copy(sources[i], held[i], sems.at[i]) for i in range(count)]
    outs = [pltpu.make_async_copy(held[i], results[i], sems.at[count + i]) for i in range(count)]
    for copy in ins:
        copy.start()
    for come, go in zip(ins, outs):
        come.wait()
        go.start()
    for copy in outs:
        copy.wait()


def body(
    efield_north,
    efield_east,
    efield_up,
    hfield_north,
    hfield_east,
    hfield_up,
    sigma_profile,
    flash_lat,
    flash_lon,
    flash_step,
    flash_amp,
):
    rows, width = efield_north.shape
    layers = sigma_profile.shape[0]
    n_lat, n_lon = lax.axis_size("lat"), lax.axis_size("lon")
    lat_count, lon_count = rows * n_lat, (width // layers) * n_lon
    dims = (
        n_lat,
        n_lon,
        layers,
        time_step(lat_count, lon_count),
        RADIUS_CELLS * math.pi / lat_count,
    )
    wide, tall = width + 2 * HALO_LANES, rows + 2 * HALO_ROWS
    f32 = jnp.float32
    vmem = pl.BlockSpec(memory_space=pltpu.VMEM)
    field = jax.ShapeDtypeStruct((rows, width), f32)
    dma = pltpu.SemaphoreType.DMA
    hbm = pl.BlockSpec(memory_space=pltpu.HBM)
    strokes = flash_lat.shape[0]
    outs = [field] * 6 + [jax.ShapeDtypeStruct((STEPS, 2, layers, rows), f32)]
    results = pl.pallas_call(
        functools.partial(kernel, dims),
        out_shape=outs,
        in_specs=[hbm] * 12,
        out_specs=[vmem] * 7,
        scratch_shapes=[
            pltpu.VMEM((6, tall + 2 * PAD, wide), f32),
            pltpu.VMEM((6, tall + 2 * PAD, wide), f32),
            pltpu.VMEM((10, tall, 128), f32),
            pltpu.VMEM((5, 8, wide), f32),
            pltpu.VMEM((STEPS * tall, wide), f32),
            pltpu.VMEM((8, 128), f32),
            pltpu.VMEM((rows, 128), f32),
            pltpu.VMEM((n_lon, rows, 128), f32),
            pltpu.VMEM((3, tall + 2 * PAD, 128), f32),
            pltpu.VMEM((3, tall + 2 * PAD, 128), f32),
            pltpu.VMEM((tall + 2 * PAD, 128), f32),
            pltpu.VMEM((1, layers), f32),
            pltpu.VMEM((1, strokes), jnp.int32),
            pltpu.VMEM((1, strokes), jnp.int32),
            pltpu.VMEM((1, strokes), jnp.int32),
            pltpu.VMEM((1, strokes), f32),
            pltpu.VMEM((tall, 128), f32),
            dma((12,)),
            dma((8,)), dma((8,)), dma((8,)), dma((8,)),
            dma((n_lon,)), dma((n_lon,)), dma((2,)), dma((2,)),
        ],
        compiler_params=pltpu.CompilerParams(
            collective_id=0, has_side_effects=True, vmem_limit_bytes=VMEM_GRANT
        ),
    )(
        efield_north,
        efield_east,
        efield_up,
        hfield_north,
        hfield_east,
        hfield_up,
        sigma_profile[None, :],
        flash_lat[None, :],
        flash_lon[None, :],
        flash_step[None, :],
        flash_amp[None, :],
        jnp.asarray(row_table(lat_count, lon_count)),
    )
    results = pl.pallas_call(
        hand_over,
        out_shape=outs,
        in_specs=[hbm] * 7,
        out_specs=[hbm] * 7,
        scratch_shapes=[pltpu.VMEM(x.shape, x.dtype) for x in outs] + [dma((14,))],
        compiler_params=pltpu.CompilerParams(vmem_limit_bytes=VMEM_GRANT),
    )(*results)
    return (*results[:6], jnp.transpose(results[6], (0, 1, 3, 2)))


def solution(mesh):
    fields = P("lat", "lon")
    return jax.shard_map(
        body,
        mesh=mesh,
        in_specs=(fields,) * 6 + (P(),) * 5,
        out_specs=(fields,) * 6 + (P(None, None, "lat", None),),
        check_vma=False,
    )
```

```python
import functools
import math

import jax
import jax.numpy as jnp
import numpy as np
from jax import lax
from jax.experimental import pallas as pl
from jax.experimental.pallas import tpu as pltpu
from jax.sharding import PartitionSpec as P

CHANNEL = 3
STEPS = 9
RADIUS_CELLS = 1529.0
COURANT = 0.9
VMEM_GRANT = 63 * 1024 * 1024

HALO_ROWS = 8
HALO_LANES = 128
PAD = 8
FIRST = 5
MESH = pl.DeviceIdType.MESH
DIRECTIONS = [(a, b) for a in (-1, 0, 1) for b in (-1, 0, 1) if (a, b) != (0, 0)]
EN, EE, EU, HN, HE, HR = range(6)
(C_AS, C_BE, C_CN, C_DU, C_DT, C_GC, C_IC, C_JN, C_KL, C_LY) = range(10)
C_KEEP = 10


def time_step(lat_count, lon_count):
    lon_angle = 2.0 * math.pi / lon_count
    lat_angle = math.pi / lat_count
    narrowest = RADIUS_CELLS * lon_angle * math.sin(lat_angle)
    lat_length = RADIUS_CELLS * lat_angle
    return COURANT / math.sqrt(1.0 / narrowest**2 + 1.0 / lat_length**2 + 1.0)


def row_table(lat_count, lon_count):
    f = np.float32
    lon_angle = 2.0 * math.pi / lon_count
    lat_angle = math.pi / lat_count
    dt = time_step(lat_count, lon_count)
    ly = RADIUS_CELLS * math.pi / lat_count
    row = np.arange(lat_count)
    centre = f(-0.5 * math.pi) + (row.astype(f) + f(0.5)) * f(lat_angle)
    north = centre + f(0.5 * lat_angle)
    south = centre - f(0.5 * lat_angle)
    following = centre + f(lat_angle)
    pole = row == lat_count - 1
    scale = RADIUS_CELLS * lon_angle
    band = 2.0 * RADIUS_CELLS * scale * math.sin(0.5 * lat_angle)
    lc = f(scale) * np.cos(centre)
    ln = f(scale) * np.cos(following)
    le = np.where(pole, f(0), f(scale) * np.cos(north))
    ls = np.where(row == 0, f(0), f(scale) * np.cos(south))
    ls[-1] = le[-2]
    ac = f(band) * np.cos(centre)
    ae = np.where(pole, f(1), f(band) * np.cos(north))
    se = np.where(pole, f(1), le)
    keep = np.where(pole, f(0), f(1))
    table = np.zeros((lat_count + 2 * HALO_ROWS, 128), f)
    inner = table[HALO_ROWS:-HALO_ROWS]
    inner[:, C_AS] = dt * ls / ac
    inner[:, C_BE] = dt * le / ac
    inner[:, C_CN] = dt * ly / ac
    inner[:, C_DU] = keep * dt / se
    inner[:, C_DT] = keep * dt
    inner[:, C_GC] = 1.0 / lc
    inner[:, C_IC] = keep * lc / ae
    inner[:, C_JN] = keep * ln / ae
    inner[:, C_KL] = keep * ly / ae
    inner[:, C_LY] = keep / ly
    inner[:, C_KEEP] = keep
    return table


def turn(x, by):
    return pltpu.roll(x, by % x.shape[1], 1)


def div24(x):
    return lax.shift_right_logical(x * 2731, 16)


def kernel(
    dims,
    en, ee, eu, hn, he, hr, h_sigma, h_lat, h_lon, h_step, h_amp, h_table,
    o_en, o_ee, o_eu, o_hn, o_he, o_hr, o_zon,
    ext_a, ext_b, coef, lanes, src, small, sums_out, sums_in, zon_cap, zon_out, strip,
    sigma, f_lat, f_lon, f_step, f_amp, table,
    load, send_a, recv_a, send_b, recv_b, send_s, recv_s, send_z, recv_z,
):
    n_lat, n_lon, layers, dt, ly = dims
    rows, width = en.shape
    strokes = h_lat.shape[1]
    wide = width + 2 * HALO_LANES
    tall = rows + 2 * HALO_ROWS
    groups = tall // 8
    vregs = wide // 128
    lat, lon = lax.axis_index("lat"), lax.axis_index("lon")
    own_r = pl.ds(PAD + HALO_ROWS, rows)
    own_c = pl.ds(HALO_LANES, width)

    def at(a, b):
        row = jnp.clip(lat + a, 0, n_lat - 1) if a else lat
        return {"lat": row, "lon": lax.rem(lon + b + n_lon, n_lon)}

    def there(a):
        return lat + a >= 0 if a < 0 else lat + a < n_lat

    def guarded(a, fn):
        if a == 0:
            fn()
        else:
            pl.when(there(a))(fn)

    loads = [
        pltpu.make_async_copy(x, ext_a.at[f, own_r, own_c], load.at[f])
        for f, x in enumerate((en, ee, eu, hn, he, hr))
    ]
    here_rows = h_table.at[pl.ds(pl.multiple_of(lat * rows, 8), tall), :]
    pairs = (
        (here_rows, table), (h_sigma, sigma), (h_lat, f_lat), (h_lon, f_lon),
        (h_step, f_step), (h_amp, f_amp),
    )
    loads += [pltpu.make_async_copy(x, y, load.at[6 + i]) for i, (x, y) in enumerate(pairs)]
    for copy in loads:
        copy.start()

    barrier = pltpu.get_barrier_semaphore()

    def greet(a, b):
        pl.semaphore_signal(barrier, inc=1, device_id=at(a, b), device_id_type=MESH)

    for k in range(1, n_lon):
        greet(0, k)
    for a in (-1, 1):
        def both(a=a):
            for b in (-1, 0, 1):
                greet(a, b)
        pl.when(there(a))(both)

    low = PAD + HALO_ROWS
    for ext in (ext_a, ext_b):
        edge = jnp.zeros((6, 8, wide), jnp.float32)
        ext[:, 0:PAD, :] = edge
        ext[:, low + rows + 8:, :] = edge
        for a, first_row in ((-1, PAD), (1, low + rows)):
            def clear(ext=ext, first_row=first_row):
                ext[:, first_row:first_row + 8, :] = jnp.zeros((6, 8, wide), jnp.float32)
            pl.when(jnp.logical_not(there(a)))(clear)
    for copy in loads:
        copy.wait()
    last = pl.ds(low + rows - 8, 8)
    keep = jnp.broadcast_to(table[HALO_ROWS + rows - 8:HALO_ROWS + rows, C_KEEP:C_KEEP + 1], (8, width))
    for f in (EE, EU, HN):
        ext_a[f, last, own_c] = keep * ext_a[f, last, own_c]

    def fold(x):
        for by in (width // 2, width // 4, width // 8, width // 16):
            x = x + turn(x, by)
        return x[:, :128] * (1.0 / (n_lon * (width // layers)))

    lane = lax.broadcasted_iota(jnp.int32, (rows, 128), 1)
    sums_out[...] = jnp.where(
        lane < layers,
        fold(ext_a[EE, own_r, own_c]),
        jnp.where(lane < 2 * layers, fold(ext_a[HN, own_r, own_c]), fold(ext_a[HR, own_r, own_c])),
    )

    greeted = (n_lon - 1) + 3 * (lat > 0).astype(jnp.int32) + 3 * (lat < n_lat - 1).astype(jnp.int32)
    pl.semaphore_wait(barrier, greeted)

    def strip_copy(src_ref, dst_ref, sends, recvs, i):
        a, b = DIRECTIONS[i]
        depth = FIRST if dst_ref is ext_a else STEPS - FIRST
        def part(first, size, halo, d, side):
            if d == 0:
                return pl.ds(first, size)
            if side == 0:
                return pl.ds(first + size - halo, halo) if d > 0 else pl.ds(first, halo)
            return pl.ds(first - halo, halo) if d > 0 else pl.ds(first + size, halo)
        def cut(side):
            return (
                slice(None),
                part(PAD + HALO_ROWS, rows, depth, a, side),
                part(HALO_LANES, width, HALO_LANES, b, side),
            )
        return pltpu.make_async_remote_copy(
            src_ref=src_ref.at[cut(0)],
            dst_ref=dst_ref.at[cut(1)],
            send_sem=sends.at[i],
            recv_sem=recvs.at[i],
            device_id=at(a, b),
            device_id_type=MESH,
        )

    def start_all(*args):
        for i, (a, b) in enumerate(DIRECTIONS):
            guarded(a, lambda i=i: strip_copy(*args, i).start())

    def wait_sends(*args):
        for i, (a, b) in enumerate(DIRECTIONS):
            guarded(a, lambda i=i: strip_copy(*args, i).wait_send())

    def wait_recvs(*args):
        for i, (a, b) in enumerate(DIRECTIONS):
            guarded(-a, lambda i=i: strip_copy(*args, i).wait_recv())

    first = (ext_a, ext_a, send_a, recv_a)
    second = (ext_a, ext_b, send_b, recv_b)

    def sum_copy(k):
        return pltpu.make_async_remote_copy(
            src_ref=sums_out,
            dst_ref=sums_in.at[k],
            send_sem=send_s.at[k],
            recv_sem=recv_s.at[k],
            device_id=at(0, k),
            device_id_type=MESH,
        )

    for k in range(1, n_lon):
        sum_copy(k).start()
    start_all(*first)

    rows_tab = table[...]
    for c in range(10):
        coef[c] = jnp.broadcast_to(rows_tab[:, c:c + 1], (tall, 128))
    small[...] = jnp.zeros((8, 128), jnp.float32)
    small[0:1, 0:layers] = sigma[...]
    one = jnp.broadcast_to(small[0:1, :], (8, 128))
    pair = one + turn(one, 24)
    sig = pair + turn(pair, 48) + turn(one, 96)
    half = 0.5 * dt * sig
    dec = (1.0 - half) / (1.0 + half)
    drv = dt / (1.0 + half)
    lane8 = lax.broadcasted_iota(jnp.int32, (8, 128), 1)

    def spread(x):
        out = []
        for v in range(vregs):
            off = (8 * v - 8) % 24
            out.append(jnp.where(lane8 < 96, turn(x, -off), turn(x, 24 - off)))
        return jnp.concatenate(out, axis=1)

    at_lane = lax.broadcasted_iota(jnp.int32, (8, wide), 1) + 16
    layer = at_lane - 24 * div24(at_lane)
    lanes[0] = spread(dec)
    lanes[1] = spread(drv)
    lanes[2] = jnp.where(layer < CHANNEL, lanes[1], 0.0)
    lanes[3] = jnp.where(layer == layers - 1, 0.0, 1.0)
    lanes[4] = jnp.where(layer == 0, 0.0, 1.0)

    place = lax.broadcasted_iota(jnp.int32, (wide, strokes), 0) + 16
    cell = div24(place) - 6 + lon * (width // layers)
    total_lon = n_lon * (width // layers)
    cell = jnp.where(cell < 0, cell + total_lon, cell)
    cell = jnp.where(cell >= total_lon, cell - total_lon, cell)
    cells = (cell == f_lon[...]).astype(jnp.float32).astype(jnp.bfloat16)
    row_no = lax.broadcasted_iota(jnp.int32, (tall, strokes), 0) + (lat * rows - HALO_ROWS)
    in_row = jnp.where(row_no == f_lat[...], jnp.broadcast_to(f_amp[...], (tall, strokes)), 0.0)
    def sources(s, carry):
        amps = jnp.where(f_step[...] == s, in_row, 0.0)
        total = None
        for _ in range(3):
            part = amps.astype(jnp.bfloat16)
            amps = amps - part.astype(jnp.float32)
            term = lax.dot_general(
                part, cells, (((1,), (1,)), ((), ())), preferred_element_type=jnp.float32
            )
            total = term if total is None else total + term
        src[pl.ds(pl.multiple_of(s * tall, 8), tall), :] = total
        return carry
    lax.fori_loop(0, FIRST, sources, 0)

    for k in range(1, n_lon):
        sum_copy(k).wait()
    mean = sums_out[...]
    for k in range(1, n_lon):
        mean = mean + sums_in[k]
    strip[own_r, :] = mean
    strip[0:low, :] = jnp.zeros((low, 128), jnp.float32)

    def zone_copy(a):
        i = 0 if a < 0 else 1
        return pltpu.make_async_remote_copy(
            src_ref=strip.at[pl.ds(low, 8) if a < 0 else pl.ds(low + rows - 8, 8), :],
            dst_ref=sums_in.at[0, pl.ds(8, 8) if a < 0 else pl.ds(0, 8), :],
            send_sem=send_z.at[i],
            recv_sem=recv_z.at[i],
            device_id=at(a, 0),
            device_id_type=MESH,
        )

    for a in (-1, 1):
        guarded(a, lambda a=a: zone_copy(a).start())

    def unpack(x):
        out = []
        lane_no = lax.broadcasted_iota(jnp.int32, x.shape, 1)
        for f in range(3):
            y = jnp.where(lane_no < layers, turn(x, -layers * f), 0.0)
            p = y + turn(y, 24)
            out.append(p + turn(p, 48) + turn(y, 96))
        return out

    zero_low = jnp.zeros((3, low, 128), jnp.float32)
    zon_cap[:, 0:low, :] = zero_low
    zon_cap[:, low + rows:, :] = zero_low
    zon_out[:, 0:low, :] = zero_low
    zon_out[:, low + rows:, :] = zero_low
    for f, z in enumerate(unpack(mean)):
        zon_cap[f, own_r, :] = z
        zon_out[f, own_r, :] = z

    z_dec, z_drv, z_top, z_bot = [lanes.at[i, :, 128:256] for i in (0, 1, 3, 4)]

    def zonal_step(zon, span):
        for g in span:
            lo, r = PAD + 8 * g, 8 * g
            east = zon[0, lo:lo + 8, :]
            zon[2, lo:lo + 8, :] = (
                zon[2, lo:lo + 8, :]
                - coef[C_AS, r:r + 8] * zon[0, lo - 1:lo + 7, :]
                + coef[C_BE, r:r + 8] * east
            )
            zon[1, lo:lo + 8, :] = zon[1, lo:lo + 8, :] - coef[C_DT, r:r + 8] * (
                z_top[...] * turn(east, -1) - east
            )
        for g in span:
            lo, r = PAD + 8 * g, 8 * g
            up, north = zon[2, lo:lo + 8, :], zon[1, lo:lo + 8, :]
            zon[0, lo:lo + 8, :] = z_dec[...] * zon[0, lo:lo + 8, :] + z_drv[...] * (
                coef[C_LY, r:r + 8] * (zon[2, lo + 1:lo + 9, :] - up)
                - (north - z_bot[...] * turn(north, 1))
            )

    def rowc(c, g):
        return jnp.concatenate([coef[c, 8 * g:8 * g + 8]] * vregs, axis=1)

    def step(ext, s):
        zonal_step(zon_cap, range(1, groups - 1))
        for g in range(groups):
            lo = PAD + 8 * g
            here = slice(lo, lo + 8)
            south = slice(lo - 1, lo + 7)
            top = lanes[3]
            e_n, e_e, e_u = ext[EN, here], ext[EE, here], ext[EU, here]
            up = (
                ext[HR, here]
                - rowc(C_AS, g) * ext[EE, south]
                + rowc(C_BE, g) * e_e
                - rowc(C_CN, g) * (turn(e_n, -layers) - e_n)
            )
            if g in (1, groups - 2):
                row = lax.broadcasted_iota(jnp.int32, (8, wide), 0) + (lat * rows - HALO_ROWS + 8 * g)
                pole = 0 if g == 1 else n_lat * rows - 1
                up = jnp.where(row == pole, spread(zon_cap[2, here]), up)
            ext[HR, here] = up
            ext[HN, here] = (
                ext[HN, here]
                - rowc(C_DU, g) * (e_u - turn(e_u, -layers))
                - rowc(C_DT, g) * (top * turn(e_e, -1) - e_e)
            )
            ext[HE, here] = (
                ext[HE, here]
                - (dt / ly) * (e_u - ext[EU, south])
                + dt * (top * turn(e_n, -1) - e_n)
            )
        for g in range(groups):
            lo = PAD + 8 * g
            here = slice(lo, lo + 8)
            north = slice(lo + 1, lo + 9)
            decay, drive, channel, bot = lanes[0], lanes[1], lanes[2], lanes[4]
            h_n, h_e, h_r = ext[HN, here], ext[HE, here], ext[HR, here]
            ext[EN, here] = decay * ext[EN, here] + drive * (
                h_e - bot * turn(h_e, 1) - rowc(C_GC, g) * (h_r - turn(h_r, layers))
            )
            ext[EE, here] = decay * ext[EE, here] + drive * (
                rowc(C_LY, g) * (ext[HR, north] - h_r) - (h_n - bot * turn(h_n, 1))
            )
            ext[EU, here] = (
                decay * ext[EU, here]
                + drive
                * (
                    rowc(C_IC, g) * h_e
                    - rowc(C_JN, g) * ext[HE, north]
                    + rowc(C_KL, g) * (h_n - turn(h_n, layers))
                )
                + channel * src[pl.ds(pl.multiple_of(s * tall + 8 * g, 8), 8), :]
            )

    def steps(ext, begin, end):
        def one_step(s, carry):
            step(ext, s)
            return carry
        lax.fori_loop(begin, end, one_step, 0)

    wait_recvs(*first)
    wait_sends(*first)
    steps(ext_a, 0, FIRST)
    start_all(*second)
    ext_b[:, own_r, own_c] = ext_a[:, own_r, own_c]

    lax.fori_loop(FIRST, STEPS, sources, 0)
    for a in (-1, 1):
        def take(a=a):
            zone_copy(a).wait_recv()
            side = unpack(sums_in[0, 0:8, :] if a > 0 else sums_in[0, 8:16, :])
            for f in range(3):
                if a > 0:
                    zon_out[f, PAD:low, :] = side[f]
                else:
                    zon_out[f, low + rows:low + rows + 8, :] = side[f]
        guarded(-a, take)
        guarded(a, lambda a=a: zone_copy(a).wait_send())

    def record(s, carry):
        both = jnp.where(lane < layers, zon_out[0, own_r, :], turn(zon_out[2, own_r, :], layers))
        both = jnp.transpose(both)
        o_zon[s, 0] = both[0:layers]
        o_zon[s, 1] = both[layers:2 * layers]
        zonal_step(zon_out, range(groups))
        return carry
    lax.fori_loop(0, STEPS, record, 0)

    wait_recvs(*second)
    steps(ext_b, FIRST, STEPS)
    for f, out in ((EN, o_en), (EE, o_ee), (EU, o_eu), (HN, o_hn), (HE, o_he), (HR, o_hr)):
        out[...] = ext_b[f, own_r, own_c]
    wait_sends(*second)


def hand_over(*refs):
    count = len(refs) // 3
    sources, results, held, sems = refs[:count], refs[count:2 * count], refs[2 * count:-1], refs[-1]
    ins = [pltpu.make_async_copy(sources[i], held[i], sems.at[i]) for i in range(count)]
    outs = [pltpu.make_async_copy(held[i], results[i], sems.at[count + i]) for i in range(count)]
    for copy in ins:
        copy.start()
    for come, go in zip(ins, outs):
        come.wait()
        go.start()
    for copy in outs:
        copy.wait()


def body(
    efield_north,
    efield_east,
    efield_up,
    hfield_north,
    hfield_east,
    hfield_up,
    sigma_profile,
    flash_lat,
    flash_lon,
    flash_step,
    flash_amp,
):
    rows, width = efield_north.shape
    layers = sigma_profile.shape[0]
    n_lat, n_lon = lax.axis_size("lat"), lax.axis_size("lon")
    lat_count, lon_count = rows * n_lat, (width // layers) * n_lon
    dims = (
        n_lat,
        n_lon,
        layers,
        time_step(lat_count, lon_count),
        RADIUS_CELLS * math.pi / lat_count,
    )
    wide, tall = width + 2 * HALO_LANES, rows + 2 * HALO_ROWS
    f32 = jnp.float32
    vmem = pl.BlockSpec(memory_space=pltpu.VMEM)
    field = jax.ShapeDtypeStruct((rows, width), f32)
    dma = pltpu.SemaphoreType.DMA
    hbm = pl.BlockSpec(memory_space=pltpu.HBM)
    strokes = flash_lat.shape[0]
    outs = [field] * 6 + [jax.ShapeDtypeStruct((STEPS, 2, layers, rows), f32)]
    results = pl.pallas_call(
        functools.partial(kernel, dims),
        out_shape=outs,
        in_specs=[hbm] * 12,
        out_specs=[vmem] * 7,
        scratch_shapes=[
            pltpu.VMEM((6, tall + 2 * PAD, wide), f32),
            pltpu.VMEM((6, tall + 2 * PAD, wide), f32),
            pltpu.VMEM((10, tall, 128), f32),
            pltpu.VMEM((5, 8, wide), f32),
            pltpu.VMEM((STEPS * tall, wide), f32),
            pltpu.VMEM((8, 128), f32),
            pltpu.VMEM((rows, 128), f32),
            pltpu.VMEM((n_lon, rows, 128), f32),
            pltpu.VMEM((3, tall + 2 * PAD, 128), f32),
            pltpu.VMEM((3, tall + 2 * PAD, 128), f32),
            pltpu.VMEM((tall + 2 * PAD, 128), f32),
            pltpu.VMEM((1, layers), f32),
            pltpu.VMEM((1, strokes), jnp.int32),
            pltpu.VMEM((1, strokes), jnp.int32),
            pltpu.VMEM((1, strokes), jnp.int32),
            pltpu.VMEM((1, strokes), f32),
            pltpu.VMEM((tall, 128), f32),
            dma((12,)),
            dma((8,)), dma((8,)), dma((8,)), dma((8,)),
            dma((n_lon,)), dma((n_lon,)), dma((2,)), dma((2,)),
        ],
        compiler_params=pltpu.CompilerParams(
            collective_id=0, has_side_effects=True, vmem_limit_bytes=VMEM_GRANT
        ),
    )(
        efield_north,
        efield_east,
        efield_up,
        hfield_north,
        hfield_east,
        hfield_up,
        sigma_profile[None, :],
        flash_lat[None, :],
        flash_lon[None, :],
        flash_step[None, :],
        flash_amp[None, :],
        jnp.asarray(row_table(lat_count, lon_count)),
    )
    results = pl.pallas_call(
        hand_over,
        out_shape=outs,
        in_specs=[hbm] * 7,
        out_specs=[hbm] * 7,
        scratch_shapes=[pltpu.VMEM(x.shape, x.dtype) for x in outs] + [dma((14,))],
        compiler_params=pltpu.CompilerParams(vmem_limit_bytes=VMEM_GRANT),
    )(*results)
    return (*results[:6], jnp.transpose(results[6], (0, 1, 3, 2)))


def solution(mesh):
    fields = P("lat", "lon")
    return jax.shard_map(
        body,
        mesh=mesh,
        in_specs=(fields,) * 6 + (P(),) * 5,
        out_specs=(fields,) * 6 + (P(None, None, "lat", None),),
        check_vma=False,
    )
```
